512 devices in a mesh: segment: 32 (over z, core), head: 16 (over y, x).
Axes of the slice: x: 4, y: 4, z: 16, core: 2. Of those that a mesh axis runs over, the one named last changes fastest.
Arguments:
- slices: bfloat16 [4096, 4096], P('segment', 'head'), may hold values from -6 to 6
- new_slice: bfloat16 [128, 4096], P(None, 'head'), may hold values from -6 to 6
- norm_gain: float32 [32, 4096], P('segment'), may hold values from 0.1 to 1.9
- w_query: bfloat16 [32, 4096, 2048], P('segment', None, 'head'), may hold values from -0.09375 to 0.09375
- w_keyval: bfloat16 [32, 4096, 1024], P('segment', None, 'head'), may hold values from -0.1875 to 0.1875
- w_out: bfloat16 [32, 2048, 4096], P('segment', 'head'), may hold values from -0.375 to 0.375
- cached_rows: bfloat16 [32, 16384, 256], P('segment', 'head'), may hold values from -400 to 400
- lengths: int32 [32], P('segment'), may hold values from 256 to 4096
Outputs:
- first_pass: float32 [4096, 4096], P('segment', 'head')
- second_pass: float32 [4096, 4096], P('segment', 'head')
The draws below stay inside these ranges and needn't reach their ends.
All inputs are finite; a program needn't handle non-finite values.
Results may differ from the reference program's by a relative error of at most 0.029.
The reference program's roundings to bfloat16 on the way (of `normed`, `queries`, `weights` and `attended`) count: a program that leaves them out, or rounds other values in their place, can miss the bound.
Values may be sent and summed in bfloat16 or wider, within the bound.
No kernel may reach another device: no remote copies, remote signals or barrier semaphores. Data moves between devices by JAX's collectives and lax.ppermute only.
A program may use at most 64 MiB of HBM per device.

```python
import jax
import jax.numpy as jnp
from jax import lax

D = 4096
H = 16
KVH = 4
HD = 128
ROWS = 128
CMAX = 4096
SEGMENTS = 32
N_SEGMENT = 32


def draw_cached_rows(key, part):
    base_key = jax.random.fold_in(key, 101)
    shape = (SEGMENTS, KVH, CMAX, 2 * HD)
    base = jnp.clip(2.0 * jax.random.normal(base_key, shape, jnp.float32), -12.0, 12.0)
    return base.reshape(SEGMENTS, KVH * CMAX, 2 * HD).astype(jnp.bfloat16)


def plant(drawn, own_key, smallest, top_value):
    shape = drawn.shape
    spot = [jax.random.randint(jax.random.fold_in(own_key, axis), (), 0, shape[axis]) for axis in range(len(shape))]
    drawn = drawn.at[tuple(spot)].set(smallest)
    longest = shape.index(max(shape))
    spot[longest] = (spot[longest] + 1) % shape[longest]
    return drawn.at[tuple(spot)].set(top_value)


def spiked(values, stream_key, source, target, parts, factor):
    owner, partner = [(jnp.arange(values.shape[axis_at]) // (values.shape[axis_at] // parts)).reshape([-1 if axis == axis_at else 1 for axis in range(values.ndim)]) for axis_at in (source, target)]
    chosen = jax.random.permutation(stream_key, parts)[partner]
    strong = (owner == chosen) | (owner == (partner + parts // 2) % parts)
    return jnp.where(strong, factor * values, values)


def block_levels(rng, dims, split, smallest, largest):
    def one(dim, shards_of):
        draws = jax.random.uniform(jax.random.fold_in(jax.random.fold_in(rng, 6), dim), (shards_of,), jnp.float32, smallest / len(split), largest / len(split))
        return jnp.repeat(jnp.exp(draws), dims[dim] // shards_of).reshape((-1,) + (1,) * (len(dims) - dim - 1))

    factor_of = one(*split[0])
    for cut in split[1:]:
        factor_of = factor_of * one(*cut)
    return factor_of


def scatter_about(stream_key, extent, spread, reach, cuts=(), kind=jnp.bfloat16):
    values = spread * jax.random.normal(stream_key, extent, jnp.float32)
    if cuts:
        values = values * block_levels(stream_key, extent, cuts, -0.22, 0.18)
    return jnp.clip(values, -reach, reach).astype(kind)


def heavy_noise(rng, extent, deviation, most, pieces, heavy, kind=jnp.bfloat16):
    values = deviation * jax.random.normal(rng, extent, jnp.float32)
    if pieces:
        values = values * block_levels(rng, extent, pieces, -0.22, 0.18)
    return jnp.clip(spiked(values, jax.random.fold_in(rng, 3), *heavy), -most, most).astype(kind)


def setup_inputs(seed: int = 0) -> dict:
    key_list = jax.random.split(jax.random.key(seed), 9)
    slices = scatter_about(key_list[0], (SEGMENTS * ROWS, D), 1.0, 6.0, ((0, 32), (1, 16)))
    new_slice = scatter_about(key_list[1], (ROWS, D), 1.0, 6.0, ((1, 16),))
    norm_gain = jnp.clip(1.0 + 0.18 * jax.random.normal(key_list[2], (SEGMENTS, D), jnp.float32), 0.1, 1.9)
    w_query = scatter_about(key_list[3], (SEGMENTS, D, H * HD), D ** -0.5, 0.09375, ((0, 32), (2, 16)))
    w_keyval = scatter_about(key_list[4], (SEGMENTS, D, 2 * KVH * HD), (D // 4) ** -0.5, 0.1875, ((0, 32), (2, 16)))
    w_out = heavy_noise(key_list[5], (SEGMENTS, H * HD, D), (H * HD // 4) ** -0.5, 0.375, ((0, 32), (1, 16)), (1, 2, 16, 2.0))
    cached_rows = draw_cached_rows(jax.random.fold_in(key_list[8], 71), 0)
    lengths = plant(jax.random.randint(key_list[7], (SEGMENTS,), CMAX // 16, CMAX + 1), jax.random.fold_in(key_list[7], 1), CMAX // 16, CMAX).astype(jnp.int32)
    return {"slices": slices, "new_slice": new_slice, "norm_gain": norm_gain, "w_query": w_query, "w_keyval": w_keyval, "w_out": w_out, "cached_rows": cached_rows, "lengths": lengths}


EPSILON = 1e-05
ROPE_BASE = 1000000.0
NEGATIVE = -1e+30

def rotate(entries, positions):
    half_dim = entries.shape[-1] // 2
    exponent = jnp.arange(half_dim, dtype=jnp.float32) * (2.0 / entries.shape[-1])
    inverse = jnp.power(jnp.float32(ROPE_BASE), -exponent)
    angles = positions[:, None] * inverse[None, :]
    cosine = jnp.cos(angles)[:, None, :]
    sine = jnp.sin(angles)[:, None, :]
    first_half = entries[..., :half_dim]
    second_half = entries[..., half_dim:]
    return jnp.concatenate([first_half * cosine - second_half * sine, second_half * cosine + first_half * sine], axis=-1)

def normalize(rows_in, gain_vector):
    widened = rows_in.astype(jnp.float32)
    mean_square = lax.optimization_barrier(jnp.mean(widened * widened, axis=-1, keepdims=True))
    return (widened * lax.rsqrt(mean_square + EPSILON) * gain_vector).astype(jnp.bfloat16)

def section(rows_in, gain_vector, query_w, keyval_w, out_w, cache_part, length, offset, earlier_keys, earlier_values, earlier_live):
    row_count = rows_in.shape[0]
    normed = normalize(rows_in, gain_vector)
    positions = (length + offset + jnp.arange(row_count, dtype=jnp.int32)).astype(jnp.float32)
    queries = jnp.dot(normed, query_w, preferred_element_type=jnp.float32).reshape(row_count, H, HD)
    queries = rotate(queries, positions).astype(jnp.bfloat16)
    projected = jnp.dot(normed, keyval_w, preferred_element_type=jnp.float32).reshape(row_count, KVH, 2, HD)
    new_keys = rotate(projected[:, :, 0], positions).astype(jnp.bfloat16)
    new_values = projected[:, :, 1].astype(jnp.bfloat16)
    group_size = H // KVH
    cache_table = cache_part.reshape(KVH, CMAX, 2 * HD)
    cache_live = jnp.arange(CMAX, dtype=jnp.int32) < length
    row_ids = jnp.arange(row_count, dtype=jnp.int32)
    causal = row_ids[:, None] >= row_ids[None, :]
    visible = jnp.concatenate([jnp.broadcast_to(cache_live[None, :], (row_count, CMAX)), jnp.broadcast_to(jnp.asarray(earlier_live), (row_count, row_count)), causal], axis=1)
    scaling = HD ** (-0.5)

    def attend(operands):
        head_queries, cache_rows, fresh_keys, fresh_values, old_keys, old_values = operands
        key_rows = jnp.concatenate([cache_rows[:, :HD], old_keys, fresh_keys], axis=0).astype(jnp.float32)
        value_rows = jnp.concatenate([cache_rows[:, HD:], old_values, fresh_values], axis=0).astype(jnp.float32)
        scores = jnp.einsum('rgd,kd->grk', head_queries.astype(jnp.float32), key_rows) * scaling
        scores = jnp.where(visible[None], scores, NEGATIVE)
        row_peak = lax.optimization_barrier(jnp.max(scores, axis=-1, keepdims=True))
        weights = jnp.where(visible[None], jnp.exp(scores - row_peak), 0.0)
        row_total = lax.optimization_barrier(jnp.sum(weights, axis=-1, keepdims=True))
        rounded = weights.astype(jnp.bfloat16)
        summed = jnp.einsum('grk,kd->grd', rounded.astype(jnp.float32), value_rows)
        return (summed / row_total).transpose(1, 0, 2).astype(jnp.bfloat16)
    operands = (queries.reshape(row_count, KVH, group_size, HD).transpose(1, 0, 2, 3), cache_table, new_keys.transpose(1, 0, 2), new_values.transpose(1, 0, 2), earlier_keys.transpose(1, 0, 2), earlier_values.transpose(1, 0, 2))
    attended = lax.map(attend, operands).transpose(1, 0, 2, 3).reshape(row_count, H * HD)
    mixed = jnp.dot(attended, out_w, preferred_element_type=jnp.float32)
    result = rows_in.astype(jnp.float32) + mixed
    return (result, new_keys, new_values)

def reference(slices, new_slice, norm_gain, w_query, w_keyval, w_out, cached_rows, lengths):
    stacked = slices.astype(jnp.float32).reshape(N_SEGMENT, ROWS, D)
    blank_rows = jnp.zeros((ROWS, KVH, HD), jnp.bfloat16)

    def first_turn(operands):
        rows_in, gain_vector, query_w, keyval_w, out_w, cache_part, length = operands
        return section(rows_in, gain_vector, query_w, keyval_w, out_w, cache_part, length, 0, blank_rows, blank_rows, False)
    first_out, saved_keys, saved_values = lax.map(first_turn, (stacked, norm_gain, w_query, w_keyval, w_out, cached_rows, lengths))
    entering = jnp.concatenate([new_slice.astype(jnp.float32)[None], first_out[:-1]], axis=0)

    def second_turn(operands):
        rows_in, gain_vector, query_w, keyval_w, out_w, cache_part, length, old_keys, old_values = operands
        result, _, _ = section(rows_in, gain_vector, query_w, keyval_w, out_w, cache_part, length, ROWS, old_keys, old_values, True)
        return result
    second_out = lax.map(second_turn, (entering, norm_gain, w_query, w_keyval, w_out, cached_rows, lengths, saved_keys, saved_values))
    return (first_out.reshape(N_SEGMENT * ROWS, D), second_out.reshape(N_SEGMENT * ROWS, D))
```

```python
import functools

import jax
import jax.numpy as jnp
from jax import lax
from jax.experimental import pallas as pl
from jax.experimental.pallas import tpu as pltpu
from jax.sharding import PartitionSpec as P

KVH = 4
HD = 128
EPSILON = 1e-05
ROPE_BASE = 1000000.0
NEGATIVE = -1e30
BLOCK = 1024
VMEM = pl.BlockSpec(memory_space=pltpu.VMEM)
SMEM = pl.BlockSpec(memory_space=pltpu.SMEM)
PARAMS = pltpu.CompilerParams(vmem_limit_bytes=24 * 1024 * 1024)


def rope_tables(positions):
    half = HD // 2
    exponent = jnp.arange(half, dtype=jnp.float32) * (2.0 / HD)
    inverse = jnp.power(jnp.float32(ROPE_BASE), -exponent)
    angles = positions[:, None] * inverse[None, :]
    cosine = jnp.cos(angles)
    sine = jnp.sin(angles)
    return (
        jnp.concatenate([cosine, cosine], axis=1),
        jnp.concatenate([-sine, sine], axis=1),
    )


def turned(entries, cosine, sine):
    return entries * cosine + pltpu.roll(entries, HD // 2, 1) * sine


def project_kernel(x_ref, gain_ref, wq_ref, wkv_ref, cos_ref, sin_ref, q_ref, kv_ref):
    chunks, rows, part = x_ref.shape
    squares = jnp.zeros((rows, part), jnp.float32)
    for c in range(chunks):
        piece = x_ref[c].astype(jnp.float32)
        squares = squares + piece * piece
    mean_square = jnp.sum(squares, axis=1, keepdims=True) / (chunks * part)
    inverse = lax.rsqrt(mean_square + EPSILON)
    queries = jnp.zeros((rows, HD), jnp.float32)
    keyval = jnp.zeros((rows, wkv_ref.shape[1]), jnp.float32)
    for c in range(chunks):
        piece = x_ref[c].astype(jnp.float32)
        normed = (piece * inverse * gain_ref[c]).astype(jnp.bfloat16)
        span = pl.ds(c * part, part)
        queries = queries + jnp.dot(normed, wq_ref[span, :], preferred_element_type=jnp.float32)
        keyval = keyval + jnp.dot(normed, wkv_ref[span, :], preferred_element_type=jnp.float32)
    q_ref[...] = turned(queries, cos_ref[...], sin_ref[...]).astype(jnp.bfloat16)
    flipped = keyval.T
    for peer in range(kv_ref.shape[0]):
        kv_ref[peer] = flipped


def attend_kernel(second, *refs):
    if second:
        (len_ref, q_ref, kv_ref, cos_ref, sin_ref, cache_ref, wout_ref, oldk_ref, oldv_ref, y_ref) = refs
    else:
        (len_ref, q_ref, kv_ref, cos_ref, sin_ref, cache_ref, wout_ref, y_ref, newk_ref, newv_ref) = refs
    rows = q_ref.shape[0]
    length = len_ref[0]
    scaling = HD ** (-0.5)
    queries = q_ref[...]
    keyval = kv_ref[...].T
    keys = turned(keyval[:, :HD], cos_ref[...], sin_ref[...]).astype(jnp.bfloat16)
    values = keyval[:, HD:].astype(jnp.bfloat16)
    row_ids = lax.broadcasted_iota(jnp.int32, (rows, rows), 0)
    key_ids = lax.broadcasted_iota(jnp.int32, (rows, rows), 1)

    def score(key_rows):
        return (
            lax.dot_general(
                queries, key_rows, (((1,), (1,)), ((), ())), preferred_element_type=jnp.float32
            )
            * scaling
        )

    def weigh(scores, value_rows, running):
        peak, total, out = running
        joined = jnp.maximum(peak, jnp.max(scores, axis=1, keepdims=True))
        shrink = jnp.exp(peak - joined)
        weights = jnp.exp(scores - joined)
        total = shrink * total + jnp.sum(weights, axis=1, keepdims=True)
        out = shrink * out + jnp.dot(
            weights.astype(jnp.bfloat16), value_rows, preferred_element_type=jnp.float32
        )
        return (joined, total, out)

    running = (
        jnp.full((rows, 1), NEGATIVE, jnp.float32),
        jnp.zeros((rows, 1), jnp.float32),
        jnp.zeros((rows, HD), jnp.float32),
    )
    running = weigh(jnp.where(key_ids <= row_ids, score(keys), NEGATIVE), values, running)
    if second:
        running = weigh(score(oldk_ref[...]), oldv_ref[...], running)
    else:
        newk_ref[...] = keys
        newv_ref[...] = values

    def whole_block(index, running):
        span = pl.ds(pl.multiple_of(index * BLOCK, BLOCK), BLOCK)
        return weigh(score(cache_ref[span, :HD]), cache_ref[span, HD:], running)

    def last_block(index, running):
        span = pl.ds(pl.multiple_of(index * BLOCK, BLOCK), BLOCK)
        places = index * BLOCK + lax.broadcasted_iota(jnp.int32, (rows, BLOCK), 1)
        scores = jnp.where(places < length, score(cache_ref[span, :HD]), NEGATIVE)
        return weigh(scores, cache_ref[span, HD:], running)

    full = length // BLOCK
    running = lax.fori_loop(0, full, whole_block, running)
    running = lax.fori_loop(full, (length + BLOCK - 1) // BLOCK, last_block, running)
    _, total, out = running
    attended = (out / total).astype(jnp.bfloat16)
    chunks, _, part = y_ref.shape
    for c in range(chunks):
        y_ref[c] = jnp.dot(
            attended, wout_ref[:, pl.ds(c * part, part)], preferred_element_type=jnp.float32
        ).astype(jnp.bfloat16)


def local(slices, new_slice, norm_gain, w_query, w_keyval, w_out, cached_rows, lengths):
    segment_index = lax.axis_index("segment")
    head_count = lax.axis_size("head")
    rows, part = slices.shape
    group = head_count // KVH
    groups = [[g * group + i for i in range(group)] for g in range(KVH)]
    key_columns = w_keyval.shape[2]
    cosines, sines = rope_tables(
        (lengths[0] + jnp.arange(2 * rows, dtype=jnp.int32)).astype(jnp.float32)
    )
    gain = norm_gain[0].reshape(head_count, 1, part)

    cache = lax.all_to_all(
        jnp.broadcast_to(cached_rows, (group,) + cached_rows.shape[1:]),
        "head", 0, 0, axis_index_groups=groups,
    ).reshape(group * cached_rows.shape[1], 2 * HD)

    def gathered(own):
        return lax.all_to_all(
            jnp.broadcast_to(own[None], (head_count, rows, part)), "head", 0, 0
        )

    def partial_outputs(own, turn, earlier):
        cos = cosines[turn * rows : (turn + 1) * rows]
        sin = sines[turn * rows : (turn + 1) * rows]
        queries, keyval = pl.pallas_call(
            project_kernel,
            out_shape=(
                jax.ShapeDtypeStruct((rows, HD), jnp.bfloat16),
                jax.ShapeDtypeStruct((group, key_columns, rows), jnp.float32),
            ),
            in_specs=[VMEM] * 6,
            out_specs=(VMEM, VMEM),
            compiler_params=PARAMS,
            name=f"project{turn}",
        )(gathered(own), gain, w_query[0], w_keyval[0], cos, sin)
        keyval = lax.all_to_all(keyval, "head", 0, 0, axis_index_groups=groups)
        keyval = keyval.reshape(group * key_columns, rows)
        outputs = [jax.ShapeDtypeStruct((head_count, rows, part), jnp.bfloat16)]
        if not earlier:
            outputs += [jax.ShapeDtypeStruct((rows, HD), jnp.bfloat16)] * 2
        results = pl.pallas_call(
            functools.partial(attend_kernel, bool(earlier)),
            out_shape=tuple(outputs),
            in_specs=[SMEM] + [VMEM] * (6 + len(earlier)),
            out_specs=tuple([VMEM] * len(outputs)),
            compiler_params=PARAMS,
            name=f"attend{turn}",
        )(lengths, queries, keyval, cos, sin, cache, w_out[0], *earlier)
        return results[0], tuple(results[1:])

    def reduced(partials):
        arrived = lax.all_to_all(partials, "head", 0, 0)
        return jnp.sum(arrived.astype(jnp.float32), axis=0)

    partials, recent = partial_outputs(slices, 0, ())
    first_out = slices.astype(jnp.float32) + reduced(partials)
    count = lax.axis_size("segment")
    arrived = lax.ppermute(first_out, "segment", [(i, i + 1) for i in range(count - 1)])
    entering = jnp.where(segment_index == 0, new_slice.astype(jnp.float32), arrived)
    partials, _ = partial_outputs(entering.astype(jnp.bfloat16), 1, recent)
    second_out = entering + reduced(partials)
    return (first_out, second_out)


def solution(mesh):
    placed = (
        P("segment", "head"),
        P(None, "head"),
        P("segment", None),
        P("segment", None, "head"),
        P("segment", None, "head"),
        P("segment", "head", None),
        P("segment", "head", None),
        P("segment"),
    )
    return jax.shard_map(
        local,
        mesh=mesh,
        in_specs=placed,
        out_specs=(P("segment", "head"), P("segment", "head")),
        check_vma=False,
    )
```

```python
import functools

import jax
import jax.numpy as jnp
from jax import lax
from jax.experimental import pallas as pl
from jax.experimental.pallas import tpu as pltpu
from jax.sharding import PartitionSpec as P

KVH = 4
HD = 128
EPSILON = 1e-05
ROPE_BASE = 1000000.0
NEGATIVE = -1e30
HBM = pl.BlockSpec(memory_space=pltpu.HBM)
VMEM = pl.BlockSpec(memory_space=pltpu.VMEM)
SMEM = pl.BlockSpec(memory_space=pltpu.SMEM)
PARAMS = pltpu.CompilerParams(vmem_limit_bytes=24 * 1024 * 1024)


def rope_tables(positions):
    half = HD // 2
    exponent = jnp.arange(half, dtype=jnp.float32) * (2.0 / HD)
    inverse = jnp.power(jnp.float32(ROPE_BASE), -exponent)
    angles = positions[:, None] * inverse[None, :]
    cosine = jnp.cos(angles)
    sine = jnp.sin(angles)
    return (
        jnp.concatenate([cosine, cosine], axis=1),
        jnp.concatenate([-sine, sine], axis=1),
    )


def turned(entries, cosine, sine):
    return entries * cosine + pltpu.roll(entries, HD // 2, 1) * sine


def spread_kernel(in_ref, out_ref, sems):
    copies = [
        pltpu.make_async_copy(in_ref, out_ref.at[peer], sems.at[peer])
        for peer in range(out_ref.shape[0])
    ]
    for copy in copies:
        copy.start()
    for copy in copies:
        copy.wait()


def spread(block, count, name):
    return pl.pallas_call(
        spread_kernel,
        out_shape=jax.ShapeDtypeStruct((count,) + block.shape, block.dtype),
        in_specs=[VMEM],
        out_specs=HBM,
        scratch_shapes=[pltpu.SemaphoreType.DMA((count,))],
        compiler_params=PARAMS,
        name=name,
    )(block)


def project_kernel(x_ref, gain_ref, wq_ref, wkv_ref, cos_ref, sin_ref, q_ref, kv_ref):
    chunks, rows, part = x_ref.shape
    squares = jnp.zeros((rows, part), jnp.float32)
    for c in range(chunks):
        piece = x_ref[c].astype(jnp.float32)
        squares = squares + piece * piece
    mean_square = jnp.sum(squares, axis=1, keepdims=True) / (chunks * part)
    inverse = lax.rsqrt(mean_square + EPSILON)
    queries = jnp.zeros((rows, HD), jnp.float32)
    keyval = jnp.zeros((rows, wkv_ref.shape[0]), jnp.float32)
    for c in range(chunks):
        piece = x_ref[c].astype(jnp.float32)
        normed = (piece * inverse * gain_ref[c]).astype(jnp.bfloat16)
        span = pl.ds(c * part, part)
        queries = queries + jnp.dot(normed, wq_ref[span, :], preferred_element_type=jnp.float32)
        keyval = keyval + lax.dot_general(
            normed, wkv_ref[:, span], (((1,), (1,)), ((), ())), preferred_element_type=jnp.float32
        )
    q_ref[...] = turned(queries, cos_ref[...], sin_ref[...]).astype(jnp.bfloat16)
    flipped = keyval.T
    for peer in range(kv_ref.shape[0]):
        kv_ref[peer] = flipped


def score(queries, key_rows):
    return lax.dot_general(
        queries, key_rows, (((1,), (1,)), ((), ())), preferred_element_type=jnp.float32
    ) * HD ** (-0.5)


def weigh(scores, value_rows, running):
    peak, total, out = running
    joined = jnp.maximum(peak, jnp.max(scores, axis=1, keepdims=True))
    shrink = jnp.exp(peak - joined)
    weights = jnp.exp(scores - joined)
    total = shrink * total + jnp.sum(weights, axis=1, keepdims=True)
    out = shrink * out + jnp.dot(
        weights.astype(jnp.bfloat16), value_rows, preferred_element_type=jnp.float32
    )
    return (joined, total, out)


def attend_kernel(second, group, *refs):
    (place_ref, q_ref, kv_ref, cos_ref, sin_ref, wout_ref) = refs[:6]
    cache_refs = refs[6 : 6 + group]
    rest = refs[6 + group :]
    if second:
        (old_ref, y_ref, held, sems, peak_ref, total_ref, out_ref) = rest
    else:
        (y_ref, new_ref, held, sems, peak_ref, total_ref, out_ref) = rest
    rows = q_ref.shape[0]
    span = held.shape[1]
    length = place_ref[0]
    mine = place_ref[1]
    live = [length - lax.rem(mine + group - back, group) * span for back in range(group)]
    copies = [
        pltpu.make_async_copy(cache_refs[back], held.at[back], sems.at[back])
        for back in range(group)
    ]
    for back in range(group):
        pl.when(live[back] > 0)(copies[back].start)
    queries = q_ref[...]
    keyval = kv_ref[...].T
    keys = turned(keyval[:, :HD], cos_ref[...], sin_ref[...]).astype(jnp.bfloat16)
    values = keyval[:, HD:].astype(jnp.bfloat16)
    row_ids = lax.broadcasted_iota(jnp.int32, (rows, rows), 0)
    key_ids = lax.broadcasted_iota(jnp.int32, (rows, rows), 1)
    running = (
        jnp.full((rows, 1), NEGATIVE, jnp.float32),
        jnp.zeros((rows, 1), jnp.float32),
        jnp.zeros((rows, HD), jnp.float32),
    )
    scores = jnp.where(key_ids <= row_ids, score(queries, keys), NEGATIVE)
    running = weigh(scores, values, running)
    if second:
        running = weigh(score(queries, old_ref[0]), old_ref[1], running)
    else:
        new_ref[0] = keys
        new_ref[1] = values

    def keep(running):
        peak, total, out = running
        peak_ref[...] = jnp.broadcast_to(peak, (rows, HD))
        total_ref[...] = jnp.broadcast_to(total, (rows, HD))
        out_ref[...] = out

    def kept():
        return (peak_ref[...][:, :1], total_ref[...][:, :1], out_ref[...])

    keep(running)
    for back in range(group):

        @pl.when(live[back] >= span)
        def _():
            copies[back].wait()
            keep(weigh(score(queries, held[back, :, :HD]), held[back, :, HD:], kept()))

        @pl.when(jnp.logical_and(live[back] > 0, live[back] < span))
        def _():
            copies[back].wait()
            places = lax.broadcasted_iota(jnp.int32, (rows, span), 1)
            scores = jnp.where(
                places < live[back], score(queries, held[back, :, :HD]), NEGATIVE
            )
            keep(weigh(scores, held[back, :, HD:], kept()))

    _, total, out = kept()
    attended = (out / total).astype(jnp.bfloat16)
    chunks, _, part = y_ref.shape
    for c in range(chunks):
        y_ref[c] = jnp.dot(
            attended, wout_ref[:, pl.ds(c * part, part)], preferred_element_type=jnp.float32
        ).astype(jnp.bfloat16)


def local(slices, new_slice, norm_gain, w_query, w_keyval, w_out, cached_rows, lengths):
    segment_index = lax.axis_index("segment")
    head_count = lax.axis_size("head")
    rows, part = slices.shape
    group = head_count // KVH
    groups = [[g * group + i for i in range(group)] for g in range(KVH)]
    key_columns = w_keyval.shape[2]
    cosines, sines = rope_tables(
        (lengths[0] + jnp.arange(2 * rows, dtype=jnp.int32)).astype(jnp.float32)
    )
    gain = norm_gain[0].reshape(head_count, 1, part)

    def shifted(block, back):
        route = [
            (g * group + i, g * group + (i + back) % group)
            for g in range(KVH)
            for i in range(group)
        ]
        return lax.ppermute(block, "head", route)

    own_cache = cached_rows[0]
    cache = [own_cache] + [shifted(own_cache, back) for back in range(1, group)]
    place = jnp.stack([lengths[0], lax.axis_index("head") % group])
    keyval_weights = w_keyval[0].T

    def gathered(own):
        return lax.all_to_all(
            jnp.broadcast_to(own[None], (head_count, rows, part)), "head", 0, 0
        )

    def partial_outputs(everything, turn, earlier):
        cos = cosines[turn * rows : (turn + 1) * rows]
        sin = sines[turn * rows : (turn + 1) * rows]
        queries, keyval = pl.pallas_call(
            project_kernel,
            out_shape=(
                jax.ShapeDtypeStruct((rows, HD), jnp.bfloat16),
                jax.ShapeDtypeStruct((group, key_columns, rows), jnp.float32),
            ),
            in_specs=[VMEM] * 6,
            out_specs=(VMEM, VMEM),
            compiler_params=PARAMS,
            name=f"project{turn}",
        )(everything, gain, w_query[0], keyval_weights, cos, sin)
        keyval = lax.all_to_all(keyval, "head", 0, 0, axis_index_groups=groups)
        keyval = keyval.reshape(group * key_columns, rows)
        outputs = [jax.ShapeDtypeStruct((head_count, rows, part), jnp.bfloat16)]
        if not earlier:
            outputs += [jax.ShapeDtypeStruct((2, rows, HD), jnp.bfloat16)]
        square = pltpu.VMEM((rows, HD), jnp.float32)
        results = pl.pallas_call(
            functools.partial(attend_kernel, bool(earlier), group),
            out_shape=tuple(outputs),
            in_specs=[SMEM] + [VMEM] * 5 + [HBM] * group + [VMEM] * len(earlier),
            out_specs=tuple([VMEM] * len(outputs)),
            scratch_shapes=[
                pltpu.VMEM((group,) + own_cache.shape, jnp.bfloat16),
                pltpu.SemaphoreType.DMA((group,)),
                square,
                square,
                square,
            ],
            compiler_params=PARAMS,
            name=f"attend{turn}",
        )(place, queries, keyval, cos, sin, w_out[0], *cache, *earlier)
        return results[0], tuple(results[1:])

    def reduced(partials):
        arrived = lax.all_to_all(partials, "head", 0, 0)
        return jnp.sum(arrived.astype(jnp.float32), axis=0)

    gathered_first = lax.all_to_all(spread(slices, head_count, "spread_rows"), "head", 0, 0)
    partials, recent = partial_outputs(gathered_first, 0, ())
    first_out = slices.astype(jnp.float32) + reduced(partials)
    count = lax.axis_size("segment")
    arrived = lax.ppermute(first_out, "segment", [(i, i + 1) for i in range(count - 1)])
    entering = jnp.where(segment_index == 0, new_slice.astype(jnp.float32), arrived)
    partials, _ = partial_outputs(gathered(entering.astype(jnp.bfloat16)), 1, recent)
    second_out = entering + reduced(partials)
    return (first_out, second_out)


def solution(mesh):
    placed = (
        P("segment", "head"),
        P(None, "head"),
        P("segment", None),
        P("segment", None, "head"),
        P("segment", None, "head"),
        P("segment", "head", None),
        P("segment", "head", None),
        P("segment"),
    )
    return jax.shard_map(
        local,
        mesh=mesh,
        in_specs=placed,
        out_specs=(P("segment", "head"), P("segment", "head")),
        check_vma=False,
    )
```

```python
import functools

import jax
import jax.numpy as jnp
from jax import lax
from jax.experimental import pallas as pl
from jax.experimental.pallas import tpu as pltpu
from jax.sharding import PartitionSpec as P

KVH = 4
HD = 128
EPSILON = 1e-05
ROPE_BASE = 1000000.0
NEGATIVE = -1e30
VMEM = pl.BlockSpec(memory_space=pltpu.VMEM)
SMEM = pl.BlockSpec(memory_space=pltpu.SMEM)
PARAMS = pltpu.CompilerParams(vmem_limit_bytes=24 * 1024 * 1024)


def rope_tables(positions):
    half = HD // 2
    exponent = jnp.arange(half, dtype=jnp.float32) * (2.0 / HD)
    inverse = jnp.power(jnp.float32(ROPE_BASE), -exponent)
    angles = positions[:, None] * inverse[None, :]
    cosine = jnp.cos(angles)
    sine = jnp.sin(angles)
    return (
        jnp.concatenate([cosine, cosine], axis=1),
        jnp.concatenate([-sine, sine], axis=1),
    )


def turned(entries, cosine, sine):
    return entries * cosine + pltpu.roll(entries, HD // 2, 1) * sine


def project_kernel(place_ref, x_ref, gain_ref, wq_ref, wkv_ref, cos_ref, sin_ref, packed_ref):
    chunks, rows, part = x_ref.shape
    squares = jnp.zeros((rows, part), jnp.float32)
    for c in range(chunks):
        piece = x_ref[c].astype(jnp.float32)
        squares = squares + piece * piece
    mean_square = jnp.sum(squares, axis=1, keepdims=True) / (chunks * part)
    inverse = lax.rsqrt(mean_square + EPSILON)
    queries = jnp.zeros((rows, HD), jnp.float32)
    keyval = jnp.zeros((rows, wkv_ref.shape[0]), jnp.float32)
    for c in range(chunks):
        piece = x_ref[c].astype(jnp.float32)
        normed = (piece * inverse * gain_ref[c]).astype(jnp.bfloat16)
        span = pl.ds(c * part, part)
        queries = queries + jnp.dot(normed, wq_ref[span, :], preferred_element_type=jnp.float32)
        keyval = keyval + lax.dot_general(
            normed, wkv_ref[:, span], (((1,), (1,)), ((), ())), preferred_element_type=jnp.float32
        )
    queries = turned(queries, cos_ref[...], sin_ref[...]).astype(jnp.bfloat16)
    flipped = keyval.T
    high = flipped.astype(jnp.bfloat16)
    low = (flipped - high.astype(jnp.float32)).astype(jnp.bfloat16)
    columns = flipped.shape[0]
    for peer in range(packed_ref.shape[0]):
        packed_ref[peer, pl.ds(0, rows)] = queries
        packed_ref[peer, pl.ds(rows, columns)] = high
        packed_ref[peer, pl.ds(rows + columns, columns)] = low


def score(queries, key_rows):
    return lax.dot_general(
        queries, key_rows, (((1,), (1,)), ((), ())), preferred_element_type=jnp.float32
    ) * HD ** (-0.5)


def cached_kernel(place_ref, packed_ref, cache_ref, partial_ref):
    group = packed_ref.shape[0]
    rows = partial_ref.shape[1] - 8
    span = cache_ref.shape[0]
    live = place_ref[0] - place_ref[1] * span
    places = lax.broadcasted_iota(jnp.int32, (1, span), 1)
    hidden = jnp.where(places < live, 0.0, NEGATIVE)
    queries = packed_ref[:, pl.ds(0, rows), :].reshape(group * rows, HD)
    scores = score(queries, cache_ref[:, :HD]) + hidden
    peak = jnp.max(scores, axis=1, keepdims=True)
    weights = jnp.exp(scores - peak)
    total = jnp.sum(weights, axis=1, keepdims=True)
    out = jnp.dot(
        weights.astype(jnp.bfloat16), cache_ref[:, HD:], preferred_element_type=jnp.float32
    )
    for head in range(group):
        at = slice(head * rows, (head + 1) * rows)
        partial_ref[head, pl.ds(0, rows)] = out[at]
        peaks = jnp.broadcast_to(peak[at], (rows, HD)).T
        totals = jnp.broadcast_to(total[at], (rows, HD)).T
        partial_ref[head, pl.ds(rows, 4)] = peaks[:4]
        partial_ref[head, pl.ds(rows + 4, 4)] = totals[:4]


def finish_kernel(second, *refs):
    (place_ref, packed_ref, cos_ref, sin_ref, partial_ref, wout_ref) = refs[:6]
    if second:
        (old_ref, y_ref) = refs[6:]
    else:
        (y_ref, new_ref) = refs[6:]
    group = packed_ref.shape[0]
    rows = partial_ref.shape[1] - 8
    columns = (packed_ref.shape[1] - rows) // 2
    queries = packed_ref[place_ref[1], pl.ds(0, rows), :]
    keyval = jnp.concatenate(
        [
            packed_ref[peer, pl.ds(rows, columns), :].astype(jnp.float32)
            + packed_ref[peer, pl.ds(rows + columns, columns), :].astype(jnp.float32)
            for peer in range(group)
        ],
        axis=0,
    ).T
    keys = turned(keyval[:, :HD], cos_ref[...], sin_ref[...]).astype(jnp.bfloat16)
    values = keyval[:, HD:].astype(jnp.bfloat16)
    row_ids = lax.broadcasted_iota(jnp.int32, (rows, rows), 0)
    key_ids = lax.broadcasted_iota(jnp.int32, (rows, rows), 1)
    fresh = [(jnp.where(key_ids <= row_ids, score(queries, keys), NEGATIVE), values)]
    if second:
        fresh.append((score(queries, old_ref[0]), old_ref[1]))
    else:
        new_ref[0] = keys
        new_ref[1] = values
    peaks = fresh[0][0]
    for scores, _ in fresh[1:]:
        peaks = jnp.maximum(peaks, scores)
    peak = jnp.broadcast_to(jnp.max(peaks, axis=1, keepdims=True), (rows, HD))
    stats = []
    for peer in range(group):
        part_peak = jnp.broadcast_to(partial_ref[peer, pl.ds(rows, 1)], (HD, rows)).T
        part_total = jnp.broadcast_to(partial_ref[peer, pl.ds(rows + 4, 1)], (HD, rows)).T
        peak = jnp.maximum(peak, part_peak)
        stats.append((part_peak, part_total))
    total = jnp.zeros((rows, HD), jnp.float32)
    out = jnp.zeros((rows, HD), jnp.float32)
    for scores, value_rows in fresh:
        weights = jnp.exp(scores - peak)
        total = total + jnp.sum(weights, axis=1, keepdims=True)
        out = out + jnp.dot(
            weights.astype(jnp.bfloat16), value_rows, preferred_element_type=jnp.float32
        )
    for peer, (part_peak, part_total) in enumerate(stats):
        shrink = jnp.exp(part_peak - peak)
        total = total + shrink * part_total
        out = out + shrink * partial_ref[peer, pl.ds(0, rows)]
    attended = (out / total).astype(jnp.bfloat16)
    chunks, _, part = y_ref.shape
    for c in range(chunks):
        y_ref[c] = jnp.dot(
            attended, wout_ref[:, pl.ds(c * part, part)], preferred_element_type=jnp.float32
        ).astype(jnp.bfloat16)


def local(slices, new_slice, norm_gain, w_query, w_keyval, w_out, cached_rows, lengths):
    segment_index = lax.axis_index("segment")
    head_count = lax.axis_size("head")
    rows, part = slices.shape
    group = head_count // KVH
    groups = [[g * group + i for i in range(group)] for g in range(KVH)]
    key_columns = w_keyval.shape[2]
    cosines, sines = rope_tables(
        (lengths[0] + jnp.arange(2 * rows, dtype=jnp.int32)).astype(jnp.float32)
    )
    gain = norm_gain[0].reshape(head_count, 1, part)

    place = jnp.stack([lengths[0], lax.axis_index("head") % group])
    keyval_weights = w_keyval[0].T

    def gathered(own):
        return lax.all_to_all(
            jnp.broadcast_to(own[None], (head_count, rows, part)), "head", 0, 0
        )

    def partial_outputs(everything, turn, earlier):
        cos = cosines[turn * rows : (turn + 1) * rows]
        sin = sines[turn * rows : (turn + 1) * rows]
        packed = pl.pallas_call(
            project_kernel,
            out_shape=jax.ShapeDtypeStruct((group, rows + 2 * key_columns, HD), jnp.bfloat16),
            in_specs=[SMEM] + [VMEM] * 6,
            out_specs=VMEM,
            compiler_params=PARAMS,
            name=f"project{turn}",
        )(place, everything, gain, w_query[0], keyval_weights, cos, sin)
        packed = lax.all_to_all(packed, "head", 0, 0, axis_index_groups=groups)
        partial = pl.pallas_call(
            cached_kernel,
            out_shape=jax.ShapeDtypeStruct((group, rows + 8, HD), jnp.float32),
            in_specs=[SMEM, VMEM, VMEM],
            out_specs=VMEM,
            compiler_params=PARAMS,
            name=f"cached{turn}",
        )(place, packed, cached_rows[0])
        partial = lax.all_to_all(partial, "head", 0, 0, axis_index_groups=groups)
        outputs = [jax.ShapeDtypeStruct((head_count, rows, part), jnp.bfloat16)]
        if not earlier:
            outputs += [jax.ShapeDtypeStruct((2, rows, HD), jnp.bfloat16)]
        results = pl.pallas_call(
            functools.partial(finish_kernel, bool(earlier)),
            out_shape=tuple(outputs),
            in_specs=[SMEM] + [VMEM] * (5 + len(earlier)),
            out_specs=tuple([VMEM] * len(outputs)),
            compiler_params=PARAMS,
            name=f"finish{turn}",
        )(place, packed, cos, sin, partial, w_out[0], *earlier)
        return results[0], tuple(results[1:])

    def reduced(partials):
        arrived = lax.all_to_all(partials, "head", 0, 0)
        return jnp.sum(arrived.astype(jnp.float32), axis=0)

    partials, recent = partial_outputs(gathered(slices), 0, ())
    first_out = slices.astype(jnp.float32) + reduced(partials)
    count = lax.axis_size("segment")
    route = [(i, i + 1) for i in range(count - 1)]
    arrived = lax.ppermute(first_out.astype(jnp.bfloat16), "segment", route)
    entering = jnp.where(segment_index == 0, new_slice, arrived)
    partials, _ = partial_outputs(gathered(entering), 1, recent)
    second_out = entering.astype(jnp.float32) + reduced(partials)
    return (first_out, second_out)


def solution(mesh):
    placed = (
        P("segment", "head"),
        P(None, "head"),
        P("segment", None),
        P("segment", None, "head"),
        P("segment", None, "head"),
        P("segment", "head", None),
        P("segment", "head", None),
        P("segment"),
    )
    return jax.shard_map(
        local,
        mesh=mesh,
        in_specs=placed,
        out_specs=(P("segment", "head"), P("segment", "head")),
        check_vma=False,
    )
```

```python
import functools

import jax
import jax.numpy as jnp
from jax import lax
from jax.experimental import pallas as pl
from jax.experimental.pallas import tpu as pltpu
from jax.sharding import PartitionSpec as P

KVH = 4
HD = 128
EPSILON = 1e-05
ROPE_BASE = 1000000.0
NEGATIVE = -1e30
VMEM = pl.BlockSpec(memory_space=pltpu.VMEM)
SMEM = pl.BlockSpec(memory_space=pltpu.SMEM)
PARAMS = pltpu.CompilerParams(vmem_limit_bytes=24 * 1024 * 1024)


def rope_tables(positions):
    half = HD // 2
    exponent = jnp.arange(half, dtype=jnp.float32) * (2.0 / HD)
    inverse = jnp.power(jnp.float32(ROPE_BASE), -exponent)
    angles = positions[:, None] * inverse[None, :]
    return jnp.cos(angles), jnp.sin(angles)


def turned(entries, cos_ref, sin_ref, turn):
    span = pl.ds(turn * entries.shape[0], entries.shape[0])
    cosine = cos_ref[span, :]
    sine = sin_ref[span, :]
    return entries * jnp.concatenate([cosine, cosine], axis=1) + pltpu.roll(
        entries, HD // 2, 1
    ) * jnp.concatenate([-sine, sine], axis=1)


def project_kernel(
    turn, place_ref, x_ref, gain_ref, wq_ref, wkv_ref, cos_ref, sin_ref, packed_ref, own_ref
):
    chunks, rows, part = x_ref.shape
    squares = jnp.zeros((rows, part), jnp.float32)
    for c in range(chunks):
        piece = x_ref[c].astype(jnp.float32)
        squares = squares + piece * piece
    mean_square = jnp.sum(squares, axis=1, keepdims=True) / (chunks * part)
    inverse = lax.rsqrt(mean_square + EPSILON)
    queries = jnp.zeros((rows, HD), jnp.float32)
    keyval = jnp.zeros((rows, wkv_ref.shape[0]), jnp.float32)
    for c in range(chunks):
        piece = x_ref[c].astype(jnp.float32)
        normed = (piece * inverse * gain_ref[c]).astype(jnp.bfloat16)
        span = pl.ds(c * part, part)
        queries = queries + jnp.dot(normed, wq_ref[span, :], preferred_element_type=jnp.float32)
        keyval = keyval + lax.dot_general(
            normed, wkv_ref[:, span], (((1,), (1,)), ((), ())), preferred_element_type=jnp.float32
        )
    queries = turned(queries, cos_ref, sin_ref, turn).astype(jnp.bfloat16)
    flipped = keyval.T.astype(jnp.bfloat16)
    for peer in range(packed_ref.shape[0]):
        packed_ref[peer, pl.ds(0, rows)] = queries
        packed_ref[peer, pl.ds(rows, flipped.shape[0])] = flipped
    own_ref[...] = x_ref[place_ref[2]]


def score(queries, key_rows):
    return lax.dot_general(
        queries, key_rows, (((1,), (1,)), ((), ())), preferred_element_type=jnp.float32
    ) * HD ** (-0.5)


def thirds(value):
    pieces = []
    for _ in range(3):
        piece = value.astype(jnp.bfloat16).astype(jnp.float32)
        pieces.append(piece)
        value = value - piece
    return pieces


def cached_kernel(place_ref, packed_ref, cache_ref, partial_ref):
    group = packed_ref.shape[0]
    rows = partial_ref.shape[1] - 16
    span = cache_ref.shape[0]
    live = place_ref[0] - place_ref[1] * span
    places = lax.broadcasted_iota(jnp.int32, (1, span), 1)
    hidden = jnp.where(places < live, 0.0, NEGATIVE)
    queries = packed_ref[:, pl.ds(0, rows), :].reshape(group * rows, HD)
    scores = score(queries, cache_ref[:, :HD]) + hidden
    peak = jnp.max(scores, axis=1, keepdims=True)
    weights = jnp.exp(scores - peak)
    total = jnp.sum(weights, axis=1, keepdims=True)
    out = jnp.dot(
        weights.astype(jnp.bfloat16), cache_ref[:, HD:], preferred_element_type=jnp.float32
    )
    out = (out / total).astype(jnp.bfloat16)
    for head in range(group):
        at = slice(head * rows, (head + 1) * rows)
        partial_ref[head, pl.ds(0, rows)] = out[at]
        peaks = jnp.broadcast_to(peak[at], (rows, HD)).T[:8]
        totals = jnp.broadcast_to(total[at], (rows, HD)).T[:8]
        lanes = lax.broadcasted_iota(jnp.int32, (16, rows), 0)
        table = jnp.zeros((16, rows), jnp.float32)
        for at_row, piece in enumerate(thirds(peaks) + thirds(totals)):
            both = jnp.concatenate([piece, piece], axis=0)
            table = jnp.where(lanes == at_row, both, table)
        partial_ref[head, pl.ds(rows, 16)] = table.astype(jnp.bfloat16)


def finish_kernel(second, *refs):
    (place_ref, packed_ref, cos_ref, sin_ref, partial_ref, wout_ref) = refs[:6]
    if second:
        (old_ref, y_ref) = refs[6:]
    else:
        (y_ref, new_ref) = refs[6:]
    group = packed_ref.shape[0]
    rows = partial_ref.shape[1] - 16
    columns = packed_ref.shape[1] - rows
    queries = packed_ref[place_ref[1], pl.ds(0, rows), :]
    keyval = jnp.concatenate(
        [
            packed_ref[peer, pl.ds(rows, columns), :].astype(jnp.float32)
            for peer in range(group)
        ],
        axis=0,
    ).T
    keys = turned(keyval[:, :HD], cos_ref, sin_ref, int(second)).astype(jnp.bfloat16)
    values = keyval[:, HD:].astype(jnp.bfloat16)
    row_ids = lax.broadcasted_iota(jnp.int32, (rows, rows), 0)
    key_ids = lax.broadcasted_iota(jnp.int32, (rows, rows), 1)
    fresh = [(jnp.where(key_ids <= row_ids, score(queries, keys), NEGATIVE), values)]
    if second:
        fresh.append((score(queries, old_ref[0]), old_ref[1]))
    else:
        new_ref[0] = keys
        new_ref[1] = values
    peaks = fresh[0][0]
    for scores, _ in fresh[1:]:
        peaks = jnp.maximum(peaks, scores)
    peak = jnp.broadcast_to(jnp.max(peaks, axis=1, keepdims=True), (rows, HD))
    stats = []
    for peer in range(group):
        table = partial_ref[peer, pl.ds(rows, 16)].astype(jnp.float32)
        part_peak = jnp.broadcast_to(table[0:1] + table[1:2] + table[2:3], (HD, rows)).T
        part_total = jnp.broadcast_to(table[3:4] + table[4:5] + table[5:6], (HD, rows)).T
        peak = jnp.maximum(peak, part_peak)
        stats.append((part_peak, part_total))
    total = jnp.zeros((rows, HD), jnp.float32)
    out = jnp.zeros((rows, HD), jnp.float32)
    for scores, value_rows in fresh:
        weights = jnp.exp(scores - peak)
        total = total + jnp.sum(weights, axis=1, keepdims=True)
        out = out + jnp.dot(
            weights.astype(jnp.bfloat16), value_rows, preferred_element_type=jnp.float32
        )
    for peer, (part_peak, part_total) in enumerate(stats):
        shrink = jnp.exp(part_peak - peak) * part_total
        total = total + shrink
        out = out + shrink * partial_ref[peer, pl.ds(0, rows)].astype(jnp.float32)
    attended = (out / total).astype(jnp.bfloat16)
    chunks, _, part = y_ref.shape
    for c in range(chunks):
        y_ref[c] = jnp.dot(
            attended, wout_ref[:, pl.ds(c * part, part)], preferred_element_type=jnp.float32
        ).astype(jnp.bfloat16)


def reduce_kernel(parts_ref, own_ref, full_ref, *short_ref):
    summed = parts_ref[0].astype(jnp.float32)
    for c in range(1, parts_ref.shape[0]):
        summed = summed + parts_ref[c].astype(jnp.float32)
    summed = own_ref[...].astype(jnp.float32) + summed
    full_ref[...] = summed
    if short_ref:
        short_ref[0][...] = summed.astype(jnp.bfloat16)


def local(slices, new_slice, norm_gain, w_query, w_keyval, w_out, cached_rows, lengths):
    segment_index = lax.axis_index("segment")
    head_count = lax.axis_size("head")
    rows, part = slices.shape
    group = head_count // KVH
    groups = [[g * group + i for i in range(group)] for g in range(KVH)]
    key_columns = w_keyval.shape[2]
    cosines, sines = rope_tables(
        (lengths[0] + jnp.arange(2 * rows, dtype=jnp.int32)).astype(jnp.float32)
    )
    gain = norm_gain[0].reshape(head_count, 1, part)

    head_index = lax.axis_index("head")
    place = jnp.stack([lengths[0], head_index % group, head_index])
    keyval_weights = w_keyval[0].T

    def gathered(own):
        return lax.all_to_all(
            jnp.broadcast_to(own[None], (head_count, rows, part)), "head", 0, 0
        )

    def partial_outputs(everything, turn, earlier):
        packed, own = pl.pallas_call(
            functools.partial(project_kernel, turn),
            out_shape=(
                jax.ShapeDtypeStruct((group, rows + key_columns, HD), jnp.bfloat16),
                jax.ShapeDtypeStruct((rows, part), jnp.bfloat16),
            ),
            in_specs=[SMEM] + [VMEM] * 6,
            out_specs=(VMEM, VMEM),
            compiler_params=PARAMS,
            name=f"project{turn}",
        )(place, everything, gain, w_query[0], keyval_weights, cosines, sines)
        packed = lax.all_to_all(packed, "head", 0, 0, axis_index_groups=groups)
        partial = pl.pallas_call(
            cached_kernel,
            out_shape=jax.ShapeDtypeStruct((group, rows + 16, HD), jnp.bfloat16),
            in_specs=[SMEM, VMEM, VMEM],
            out_specs=VMEM,
            compiler_params=PARAMS,
            name=f"cached{turn}",
        )(place, packed, cached_rows[0])
        partial = lax.all_to_all(partial, "head", 0, 0, axis_index_groups=groups)
        outputs = [jax.ShapeDtypeStruct((head_count, rows, part), jnp.bfloat16)]
        if not earlier:
            outputs += [jax.ShapeDtypeStruct((2, rows, HD), jnp.bfloat16)]
        results = pl.pallas_call(
            functools.partial(finish_kernel, bool(earlier)),
            out_shape=tuple(outputs),
            in_specs=[SMEM] + [VMEM] * (5 + len(earlier)),
            out_specs=tuple([VMEM] * len(outputs)),
            compiler_params=PARAMS,
            name=f"finish{turn}",
        )(place, packed, cosines, sines, partial, w_out[0], *earlier)
        return results[0], own, tuple(results[1:])

    def reduced(partials, own, turn):
        outputs = [jax.ShapeDtypeStruct((rows, part), jnp.float32)]
        if turn == 0:
            outputs += [jax.ShapeDtypeStruct((rows, part), jnp.bfloat16)]
        return pl.pallas_call(
            reduce_kernel,
            out_shape=tuple(outputs),
            in_specs=[VMEM, VMEM],
            out_specs=tuple([VMEM] * len(outputs)),
            compiler_params=PARAMS,
            name=f"reduce{turn}",
        )(lax.all_to_all(partials, "head", 0, 0), own)

    opening, place, cosines, sines = lax.optimization_barrier((slices, place, cosines, sines))
    partials, own, recent = partial_outputs(gathered(opening), 0, ())
    first_out, short = reduced(partials, own, 0)
    count = lax.axis_size("segment")
    arrived = lax.ppermute(short, "segment", [(i, i + 1) for i in range(count - 1)])
    entering = jnp.where(segment_index == 0, new_slice, arrived)
    partials, own, _ = partial_outputs(gathered(entering), 1, recent)
    (second_out,) = reduced(partials, own, 1)
    return (first_out, second_out)


def solution(mesh):
    placed = (
        P("segment", "head"),
        P(None, "head"),
        P("segment", None),
        P("segment", None, "head"),
        P("segment", None, "head"),
        P("segment", "head", None),
        P("segment", "head", None),
        P("segment"),
    )
    return jax.shard_map(
        local,
        mesh=mesh,
        in_specs=placed,
        out_specs=(P("segment", "head"), P("segment", "head")),
        check_vma=False,
    )
```
